32 devices in a mesh: level: 2 (over x), gx: 4 (over z), gy: 4 (over y, core).
Axes of the slice: x: 2, y: 2, z: 4, core: 2. Of those that a mesh axis runs over, the one named last changes fastest.
Arguments:
- u_init: float32 [32, 128, 256], P('gx', 'gy'), may hold values from -6 to 6
- v_init: float32 [32, 128, 256], P('gx', 'gy'), may hold values from -6 to 6
- speed_sq: float32 [32, 128, 256], P('gx', 'gy'), may hold values from 0.25 to 1
Outputs:
- final_u: float32 [2, 32, 128, 256], P('level', 'gx', 'gy')
- final_v: float32 [2, 32, 128, 256], P('level', 'gx', 'gy')
The draws below stay inside these ranges and needn't reach their ends.
All inputs are finite; a program needn't handle non-finite values.
Results may differ from the reference program's by a relative error of at most 0.00002.
Values sent between devices are 32-bit elements; how exact they have to be, the bound alone decides.
No kernel may reach another device: no remote copies, remote signals or barrier semaphores. Data moves between devices by JAX's collectives and lax.ppermute only.
A program may use at most 64 MiB of HBM per device.

```python
import math
import jax
import jax.numpy as jnp

STEPS = 8
NX = 32
NY = 128
NZ = 256


def level_of(key, dims, cuts, least, top_value):
    def one(position, parts):
        heights = jax.random.uniform(jax.random.fold_in(jax.random.fold_in(key, 6), position), (parts,), jnp.float32, least / len(cuts), top_value / len(cuts))
        return jnp.repeat(jnp.exp(heights), dims[position] // parts).reshape((-1,) + (1,) * (len(dims) - position - 1))

    gain = one(*cuts[0])
    for cut in cuts[1:]:
        gain = gain * one(*cut)
    return gain


def normal_values(stream_key, extent, width, most, shards=(), kind=jnp.bfloat16):
    entries = width * jax.random.normal(stream_key, extent, jnp.float32)
    if shards:
        entries = entries * level_of(stream_key, extent, shards, -0.22, 0.18)
    return jnp.clip(entries, -most, most).astype(kind)


def setup_inputs(seed: int = 0) -> dict:
    splits = jax.random.split(jax.random.key(seed), 4)
    u_init = normal_values(splits[0], (NX, NY, NZ), 1.0, 6.0, ((0, 4), (1, 4)), jnp.float32)
    v_init = normal_values(splits[1], (NX, NY, NZ), 1.0, 6.0, ((0, 4), (1, 4)), jnp.float32)
    speed_sq = jnp.clip(jnp.exp(math.log(1.0) - 1.3862944 * jax.random.uniform(splits[2], (NX, NY, NZ), jnp.float32) ** level_of(splits[2], (NX, NY, NZ), ((0, 4), (1, 4)), -0.2, 0.2)), 0.25, 1.0)
    return {"u_init": u_init, "v_init": v_init, "speed_sq": speed_sq}


time_step = 0.12
half_step = 0.06
damping = 0.05


def laplace(field):
    total = -7.5 * field
    for axis in range(3):
        near = jnp.roll(field, 1, axis) + jnp.roll(field, -1, axis)
        far = jnp.roll(field, 2, axis) + jnp.roll(field, -2, axis)
        total = total + (4.0 / 3.0) * near - far / 12.0
    return total


def accel(disp, veloc, speed_sq):
    return speed_sq * laplace(disp) + damping * laplace(veloc)


def reference(u_init, v_init, speed_sq):
    pred_u, pred_v = u_init, v_init
    corr_u, corr_v = u_init, v_init
    accel_prev = accel(pred_u, pred_v, speed_sq)
    for moment in range(STEPS):
        next_u = pred_u + time_step * pred_v
        next_v = pred_v + time_step * accel_prev
        accel_next = accel(next_u, next_v, speed_sq)
        own_accel = accel(corr_u, corr_v, speed_sq)
        corr_u = corr_u + time_step * corr_v + half_step * (next_v - pred_v)
        corr_v = corr_v + time_step * own_accel + half_step * (accel_next - accel_prev)
        pred_u, pred_v, accel_prev = next_u, next_v, accel_next
    return jnp.stack([pred_u, corr_u]), jnp.stack([pred_v, corr_v])
```

```python
import functools

import jax
import jax.numpy as jnp
from jax import lax
from jax.experimental import pallas as pl
from jax.experimental.pallas import tpu as pltpu
from jax.sharding import PartitionSpec as P

STEPS = 8

time_step = 0.12
damping = 0.05
second = 0.5 * STEPS * time_step * time_step

NEAR = 4.0 / 3.0
FAR = -1.0 / 12.0

VMEM = pl.BlockSpec(memory_space=pltpu.VMEM)


def call(kernel, outs, args, flops):
    moved = 4 * (sum(a.size for a in args) + sum(o.size for o in outs))
    return pl.pallas_call(
        kernel,
        out_shape=outs,
        in_specs=[VMEM] * len(args),
        out_specs=[VMEM] * len(outs),
        compiler_params=pltpu.CompilerParams(vmem_limit_bytes=6 << 20),
        cost_estimate=pl.CostEstimate(flops=flops, bytes_accessed=moved, transcendentals=0),
    )(*args)


def spec(*shape):
    return jax.ShapeDtypeStruct(shape, jnp.float32)


def edge_specs(planes, rows, depth, count):
    pair = [spec(count * 2, rows, depth)] * 2 + [spec(count * planes, 2, depth)] * 2
    return pair


def local_lap(w_ref, out_ref):
    planes, rows, depth = w_ref.shape
    row = lax.broadcasted_iota(jnp.int32, (rows, depth), 0)
    for i in range(planes):
        w = w_ref[i]
        near = pltpu.roll(w, 1, 1) + pltpu.roll(w, depth - 1, 1)
        far = pltpu.roll(w, 2, 1) + pltpu.roll(w, depth - 2, 1)
        near += jnp.where(row >= 1, pltpu.roll(w, 1, 0), 0.0)
        near += jnp.where(row < rows - 1, pltpu.roll(w, rows - 1, 0), 0.0)
        far += jnp.where(row >= 2, pltpu.roll(w, 2, 0), 0.0)
        far += jnp.where(row < rows - 2, pltpu.roll(w, rows - 2, 0), 0.0)
        for shift in (-1, 1):
            if 0 <= i + shift < planes:
                near += w_ref[i + shift]
            if 0 <= i + 2 * shift < planes:
                far += w_ref[i + 2 * shift]
        out_ref[i] = -7.5 * w + NEAR * near + FAR * far


def edges(w_ref, x_up, x_down, y_up, y_down, part=0):
    planes, rows, _ = w_ref.shape
    a = 2 * part
    x_up[a] = NEAR * w_ref[planes - 1] + FAR * w_ref[planes - 2]
    x_up[a + 1] = FAR * w_ref[planes - 1]
    x_down[a] = FAR * w_ref[0]
    x_down[a + 1] = NEAR * w_ref[0] + FAR * w_ref[1]
    b = pl.ds(part * planes, planes)
    last, second_last = w_ref[:, rows - 1 :, :], w_ref[:, rows - 2 : rows - 1, :]
    y_up[b, 0:1, :] = NEAR * last + FAR * second_last
    y_up[b, 1:2, :] = FAR * last
    first, following = w_ref[:, 0:1, :], w_ref[:, 1:2, :]
    y_down[b, 0:1, :] = FAR * first
    y_down[b, 1:2, :] = NEAR * first + FAR * following


def finish_lap(lap_ref, x_low, x_high, y_low, y_high, part=0):
    planes, rows, _ = lap_ref.shape
    a, b = pl.ds(2 * part, 2), pl.ds(part * planes, planes)
    lap_ref[0:2] += x_low[a]
    lap_ref[planes - 2 :] += x_high[a]
    lap_ref[:, 0:2, :] += y_low[b]
    lap_ref[:, rows - 2 :, :] += y_high[b]


def first_edges(u, v, *outs):
    edges(u, *outs, part=0)
    edges(v, *outs, part=1)


def first_local(u, v, lap_u, lap_v):
    local_lap(u, lap_u)
    local_lap(v, lap_v)


def first_finish(lap_u, lap_v, v, s, xl, xh, yl, yh, q, lap, new_v, *outs):
    q[...] = lap_u[...]
    lap[...] = lap_v[...]
    finish_lap(q, xl, xh, yl, yh, part=0)
    finish_lap(lap, xl, xh, yl, yh, part=1)
    new_v[...] = v[...] + time_step * (s[...] * q[...] + damping * lap[...])
    edges(new_v, *outs)


def middle_local(new_v, u, v, q, lap, part, new_u, new_q):
    local_lap(new_v, part)
    new_u[...] = u[...] + time_step * v[...]
    new_q[...] = q[...] + time_step * lap[...]


def middle_finish(part, v, q, s, xl, xh, yl, yh, lap, new_v, *outs):
    lap[...] = part[...]
    finish_lap(lap, xl, xh, yl, yh)
    new_v[...] = v[...] + time_step * (s[...] * q[...] + damping * lap[...])
    edges(new_v, *outs)


def rate_finish(part, q, s, xl, xh, yl, yh, lap, rate, *outs):
    lap[...] = part[...]
    finish_lap(lap, xl, xh, yl, yh)
    rate[...] = s[...] * q[...] + damping * lap[...]
    edges(rate, *outs)


def last_local(scale, u, v, s, lap, rate, part, out_u, base_v):
    local_lap(rate, part)
    r = rate[...]
    out_u[...] = u[...] + time_step * v[...] + scale[0] * r
    base_v[...] = v[...] + time_step * r + scale[0] * (s[...] * lap[...])


def last_finish(scale, part, base_v, xl, xh, yl, yh, out_v):
    out_v[...] = part[...]
    finish_lap(out_v, xl, xh, yl, yh)
    out_v[...] = base_v[...] + (scale[0] * damping) * out_v[...]


def call_scaled(kernel, scale, outs, args, flops):
    moved = 4 * (sum(a.size for a in args) + sum(o.size for o in outs))
    return pl.pallas_call(
        kernel,
        out_shape=outs,
        in_specs=[pl.BlockSpec(memory_space=pltpu.SMEM)] + [VMEM] * len(args),
        out_specs=[VMEM] * len(outs),
        compiler_params=pltpu.CompilerParams(vmem_limit_bytes=6 << 20),
        cost_estimate=pl.CostEstimate(flops=flops, bytes_accessed=moved, transcendentals=0),
    )(scale, *args)


def exchange(x_up, x_down, y_up, y_down):
    def ring(axis, step):
        n = lax.axis_size(axis)
        return [(i, (i + step) % n) for i in range(n)]

    x_low = lax.ppermute(x_up, "gx", ring("gx", 1))
    x_high = lax.ppermute(x_down, "gx", ring("gx", -1))
    y_low = lax.ppermute(y_up, "gy", ring("gy", 1))
    y_high = lax.ppermute(y_down, "gy", ring("gy", -1))
    return x_low, x_high, y_low, y_high


def body(u, v, s):
    planes, rows, depth = u.shape
    block = spec(planes, rows, depth)
    work = 40 * u.size
    one = edge_specs(planes, rows, depth, 1)
    two = edge_specs(planes, rows, depth, 2)
    scale = jnp.where(lax.axis_index("level") == 0, 0.0, second).astype(jnp.float32).reshape(1)

    got = exchange(*call(first_edges, two, (u, v), u.size))
    lap_u, lap_v = call(first_local, [block] * 2, (u, v), 2 * work)
    q, lap, new_v, *sent = call(first_finish, [block] * 3 + one, (lap_u, lap_v, v, s, *got), work)
    for moment in range(1, STEPS):
        got = exchange(*sent)
        part, u, q = call(middle_local, [block] * 3, (new_v, u, v, q, lap), work)
        v = new_v
        if moment < STEPS - 1:
            lap, new_v, *sent = call(middle_finish, [block] * 2 + one, (part, v, q, s, *got), work)
        else:
            lap, rate, *sent = call(rate_finish, [block] * 2 + one, (part, q, s, *got), work)
    got = exchange(*sent)
    part, out_u, base_v = call_scaled(last_local, scale, [block] * 3, (u, v, s, lap, rate), work)
    (out_v,) = call_scaled(last_finish, scale, [block], (part, base_v, *got), work)
    return out_u[None], out_v[None]


def solution(mesh):
    placed = (P("gx", "gy", None),) * 3
    return jax.shard_map(
        body,
        mesh=mesh,
        in_specs=placed,
        out_specs=(P("level", "gx", "gy", None), P("level", "gx", "gy", None)),
        check_vma=False,
    )
```

```python
import jax
import jax.numpy as jnp
from jax import lax
from jax.experimental import pallas as pl
from jax.experimental.pallas import tpu as pltpu
from jax.sharding import PartitionSpec as P

STEPS = 8

time_step = 0.12
damping = 0.05
second = 0.5 * STEPS * time_step * time_step

NEAR = 4.0 / 3.0
FAR = -1.0 / 12.0

TILE = 8
WIDE = 6
MID = 4

VMEM = pl.BlockSpec(memory_space=pltpu.VMEM)
SMEM = pl.BlockSpec(memory_space=pltpu.SMEM)


def spec(*shape):
    return jax.ShapeDtypeStruct(shape, jnp.float32)


def call(kernel, outs, args, scalars=(), scratch=(), flops=0):
    moved = 4 * (sum(a.size for a in args) + sum(o.size for o in outs))
    return pl.pallas_call(
        kernel,
        out_shape=outs,
        in_specs=[SMEM] * len(scalars) + [VMEM] * len(args),
        out_specs=[VMEM] * len(outs),
        scratch_shapes=[pltpu.VMEM(shape, jnp.float32) for shape in scratch],
        compiler_params=pltpu.CompilerParams(vmem_limit_bytes=10 << 20),
        cost_estimate=pl.CostEstimate(flops=flops, bytes_accessed=moved, transcendentals=0),
    )(*scalars, *args)


def lap(ref, i):
    w = ref[i]
    rows, depth = w.shape
    near = ref[i - 1] + ref[i + 1]
    far = ref[i - 2] + ref[i + 2]
    near += pltpu.roll(w, 1, 1) + pltpu.roll(w, depth - 1, 1)
    far += pltpu.roll(w, 2, 1) + pltpu.roll(w, depth - 2, 1)
    near += pltpu.roll(w, 1, 0) + pltpu.roll(w, rows - 1, 0)
    far += pltpu.roll(w, 2, 0) + pltpu.roll(w, rows - 2, 0)
    return -7.5 * w + NEAR * near + FAR * far


def widen(out, width, centre, yl, yh, at, xl, xh, x_at, cl, ch, c_at):
    planes, half, depth = centre.shape
    inner = pl.ds(width, planes)
    out[inner, 0:TILE, :] = yl[pl.ds(at, planes)]
    out[inner, TILE : TILE + half, :] = centre[...]
    out[inner, TILE + half :, :] = yh[pl.ds(at, planes)]
    near = width - 2
    for side, x, c in ((0, xl, cl), (width + planes, xh, ch)):
        out[pl.ds(side, width), TILE : TILE + half, :] = x[pl.ds(x_at, width)]
        corner = side + (2 if side == 0 else 0)
        beyond = side + (0 if side == 0 else near)
        for rows in (slice(0, TILE), slice(TILE + half, None)):
            out[pl.ds(corner, near), rows, :] = c[pl.ds(c_at, near)]
            out[pl.ds(beyond, 2), rows, :] = jnp.zeros((2, TILE, depth), jnp.float32)


def pack_first(h, u, v, s, y_up, y_down, x_up, x_down):
    planes, rows, depth = u.shape
    half = rows // 2
    start = h[0] * half
    low = pl.ds(pl.multiple_of(start, TILE), TILE)
    high = pl.ds(pl.multiple_of(start + half - TILE, TILE), TILE)
    own = pl.ds(pl.multiple_of(start, TILE), half)
    at = 0
    for k, (f, width) in enumerate(((u, WIDE), (v, WIDE), (s, MID))):
        part = pl.ds(k * planes, planes)
        y_up[part] = f[:, high, :]
        y_down[part] = f[:, low, :]
        x_up[pl.ds(at, width)] = f[planes - width :, own, :]
        x_down[pl.ds(at, width)] = f[0:width, own, :]
        at += width


def pack_edges(v, q, y_up, y_down, x_up, x_down):
    planes, half, depth = v.shape
    at = 0
    for k, (f, width) in enumerate(((v, WIDE), (q, MID))):
        part = pl.ds(k * planes, planes)
        y_up[part] = f[:, half - TILE :, :]
        y_down[part] = f[:, 0:TILE, :]
        x_up[pl.ds(at, width)] = f[planes - width :]
        x_down[pl.ds(at, width)] = f[0:width]
        at += width


def pack_corners(widths, planes, yl, yh, c_up, c_down):
    depth = yl.shape[-1]
    below = lax.broadcasted_iota(jnp.int32, (TILE, depth), 0) >= TILE // 2
    at = 0
    for k, width in enumerate(widths):
        count = width - 2
        for i in range(count):
            top = k * planes + planes - count + i
            c_up[at + i] = jnp.where(below, yl[top], yh[top])
            c_down[at + i] = jnp.where(below, yl[k * planes + i], yh[k * planes + i])
        at += count


def two_steps(planes, half, v0, q0, s, v1, q1, v2, q2):
    for i in range(planes + 2 * MID):
        l = lap(v0, i + 2)
        v1[i] = v0[i + 2] + time_step * (s[i] * q0[i] + damping * l)
        if 2 <= i < planes + 2 * MID - 2:
            q1[i - 2] = q0[i] + time_step * l
    for i in range(planes + 4):
        l = lap(v1, i + 2)
        v2[i] = v1[i + 2] + time_step * (s[i + 2] * q1[i] + damping * l)
        if 2 <= i < planes + 2:
            q2[i - 2] = q1[i] + time_step * l


def third_step(planes, half, u_of, v0, v1, v2, q2, s, u_out, v_out, q_out):
    own = slice(TILE, TILE + half)
    for i in range(planes):
        l = lap(v2, i + 2)[own]
        v_out[i] = v2[i + 2, own, :] + time_step * (s[i + MID, own, :] * q2[i, own, :] + damping * l)
        q_out[i] = q2[i, own, :] + time_step * l
        moved = v0[i + WIDE, own, :] + v1[i + MID, own, :] + v2[i + 2, own, :]
        u_out[i] = u_of(i) + time_step * moved


def first_steps(h, u, v, s, yl, yh, xl, xh, cl, ch, u_out, v_out, q_out, s_wide, *rest):
    sends, (u0, v0, q0, v1, q1, v2, q2) = rest[:4], rest[4:]
    planes, rows, depth = u.shape
    half = rows // 2
    own = pl.ds(pl.multiple_of(h[0] * half, TILE), half)
    widen(u0, WIDE, u.at[:, own, :], yl, yh, 0, xl, xh, 0, cl, ch, 0)
    widen(v0, WIDE, v.at[:, own, :], yl, yh, planes, xl, xh, WIDE, cl, ch, WIDE - 2)
    widen(s_wide, MID, s.at[:, own, :], yl, yh, 2 * planes, xl, xh, 2 * WIDE, cl, ch, 2 * WIDE - 4)
    for i in range(planes + 2 * MID):
        q0[i] = lap(u0, i + 2)
    two_steps(planes, half, v0, q0, s_wide, v1, q1, v2, q2)
    third_step(
        planes, half, lambda i: u[i, own, :], v0, v1, v2, q2, s_wide, u_out, v_out, q_out
    )
    pack_edges(v_out, q_out, *sends)


def widen_both(v, q, yl, yh, xl, xh, cl, ch, v0, q0):
    planes = v.shape[0]
    widen(v0, WIDE, v, yl, yh, 0, xl, xh, 0, cl, ch, 0)
    widen(q0, MID, q, yl, yh, planes, xl, xh, WIDE, cl, ch, WIDE - 2)


def middle_steps(u, v, q, s_wide, yl, yh, xl, xh, cl, ch, u_out, v_out, q_out, *rest):
    sends, (v0, q0, v1, q1, v2, q2) = rest[:4], rest[4:]
    planes, half, depth = v.shape
    widen_both(v, q, yl, yh, xl, xh, cl, ch, v0, q0)
    two_steps(planes, half, v0, q0, s_wide, v1, q1, v2, q2)
    third_step(planes, half, lambda i: u[i], v0, v1, v2, q2, s_wide, u_out, v_out, q_out)
    pack_edges(v_out, q_out, *sends)


def last_steps(scale, u, v, q, s_wide, yl, yh, xl, xh, cl, ch, keep, send, *scratch):
    v0, q0, v1, q1, rate, l7 = scratch
    planes, half, depth = v.shape
    own = slice(TILE, TILE + half)
    widen_both(v, q, yl, yh, xl, xh, cl, ch, v0, q0)
    for i in range(planes + 2 * MID):
        l = lap(v0, i + 2)
        v1[i] = v0[i + 2] + time_step * (s_wide[i] * q0[i] + damping * l)
        if 2 <= i < planes + 2 * MID - 2:
            q1[i - 2] = q0[i] + time_step * l
    for i in range(planes + 4):
        l = lap(v1, i + 2)
        rate[i] = s_wide[i + 2] * q1[i] + damping * l
        if 2 <= i < planes + 2:
            l7[i - 2] = l[own]
    for i in range(planes):
        l = lap(rate, i + 2)[own]
        r = rate[i + 2, own, :]
        u8 = u[i] + time_step * (v[i] + v1[i + MID, own, :])
        v8 = v1[i + MID, own, :] + time_step * r
        more = s_wide[i + MID, own, :] * l7[i] + damping * l
        keep[i] = u8 + scale[0] * r
        keep[planes + i] = v8 + scale[0] * more
        send[i] = u8 + scale[1] * r
        send[planes + i] = v8 + scale[1] * more


def join(h, keep, got, out_u, out_v):
    planes, rows, depth = out_u.shape
    half = rows // 2
    own = pl.ds(pl.multiple_of(h[0] * half, TILE), half)
    other = pl.ds(pl.multiple_of((1 - h[0]) * half, TILE), half)
    for k, out in enumerate((out_u, out_v)):
        part = pl.ds(k * planes, planes)
        out[:, own, :] = keep[part]
        out[:, other, :] = got[part]


def ring(count, step):
    return [(i, (i + step) % count) for i in range(count)]


def strips(gy, step):
    def place(t):
        j, h = divmod(t % (2 * gy), 2)
        return ((h + j) % 2) * gy + j

    return [(place(t), place(t + step)) for t in range(2 * gy)]


def exchange(sends, widths, planes):
    y_up, y_down, x_up, x_down = sends
    depth = y_up.shape[-1]
    gx, gy = lax.axis_size("gx"), lax.axis_size("gy")
    xl = lax.ppermute(x_up, "gx", ring(gx, 1))
    xh = lax.ppermute(x_down, "gx", ring(gx, -1))
    yl = lax.ppermute(y_up, ("level", "gy"), strips(gy, 1))
    yh = lax.ppermute(y_down, ("level", "gy"), strips(gy, -1))
    count = sum(width - 2 for width in widths)

    def corners(*refs):
        pack_corners(widths, planes, *refs)

    c_up, c_down = call(corners, [spec(count, TILE, depth)] * 2, (yl, yh))
    cl = lax.ppermute(c_up, "gx", ring(gx, 1))
    ch = lax.ppermute(c_down, "gx", ring(gx, -1))
    return yl, yh, xl, xh, cl, ch


def edge_specs(planes, half, depth, widths):
    y = spec(len(widths) * planes, TILE, depth)
    x = spec(sum(widths), half, depth)
    return [y, y, x, x]


def body(u, v, s):
    planes, rows, depth = u.shape
    half = rows // 2
    assert lax.axis_size("level") == 2 and planes >= WIDE and half % TILE == 0
    level = lax.axis_index("level")
    h = ((level + lax.axis_index("gy")) % 2).astype(jnp.int32).reshape(1)
    mine = jnp.where(level == 0, 0.0, second).astype(jnp.float32)
    scale = jnp.stack([mine, second - mine])

    tall = half + 2 * TILE
    block = spec(planes, half, depth)
    wide = (planes + 2 * WIDE, tall, depth)
    mid = (planes + 2 * MID, tall, depth)
    thin = (planes + 4, tall, depth)
    bare = (planes, tall, depth)
    work = 100 * u.size
    first, later = (WIDE, WIDE, MID), (WIDE, MID)
    sent = edge_specs(planes, half, depth, later)

    sends = call(pack_first, edge_specs(planes, half, depth, first), (u, v, s), (h,))
    halos = exchange(sends, first, planes)
    u1, v1, q1, s_wide, *sends = call(
        first_steps,
        [block] * 3 + [spec(*mid)] + sent,
        (u, v, s, *halos),
        (h,),
        (wide, wide, mid, mid, thin, thin, bare),
        work,
    )
    halos = exchange(sends, later, planes)
    u2, v2, q2, *sends = call(
        middle_steps,
        [block] * 3 + sent,
        (u1, v1, q1, s_wide, *halos),
        (),
        (wide, mid, mid, thin, thin, bare),
        work,
    )
    halos = exchange(sends, later, planes)
    both = spec(2 * planes, half, depth)
    keep, send = call(
        last_steps,
        [both, both],
        (u2, v2, q2, s_wide, *halos),
        (scale,),
        (wide, mid, mid, thin, thin, (planes, half, depth)),
        work,
    )
    got = lax.ppermute(send, "level", ring(2, 1))
    out_u, out_v = call(join, [spec(planes, rows, depth)] * 2, (keep, got), (h,))
    return out_u[None], out_v[None]


def solution(mesh):
    placed = (P("gx", "gy", None),) * 3
    return jax.shard_map(
        body,
        mesh=mesh,
        in_specs=placed,
        out_specs=(P("level", "gx", "gy", None), P("level", "gx", "gy", None)),
        check_vma=False,
    )
```

```python
import functools

import jax
import jax.numpy as jnp
from jax import lax
from jax.experimental import pallas as pl
from jax.experimental.pallas import tpu as pltpu
from jax.sharding import PartitionSpec as P


STEPS = 8

time_step = 0.12
damping = 0.05
second = 0.5 * STEPS * time_step * time_step

NEAR = 4.0 / 3.0
FAR = -1.0 / 12.0

TILE = 8
WIDE = 6
MID = 4

FIRST = (WIDE, WIDE, MID)
LATER = (WIDE, MID)

VMEM = pl.BlockSpec(memory_space=pltpu.VMEM)
SMEM = pl.BlockSpec(memory_space=pltpu.SMEM)


def spec(*shape):
    return jax.ShapeDtypeStruct(shape, jnp.float32)


def call(kernel, outs, args, scalars=(), scratch=(), flops=0):
    moved = 4 * (sum(a.size for a in args) + sum(o.size for o in outs))
    return pl.pallas_call(
        kernel,
        out_shape=outs,
        in_specs=[SMEM] * len(scalars) + [VMEM] * len(args),
        out_specs=[VMEM] * len(outs),
        scratch_shapes=[pltpu.VMEM(shape, jnp.float32) for shape in scratch],
        compiler_params=pltpu.CompilerParams(vmem_limit_bytes=10 << 20),
        cost_estimate=pl.CostEstimate(flops=flops, bytes_accessed=moved, transcendentals=0),
    )(*scalars, *args)


def lap(ref, i):
    w = ref[i]
    rows, depth = w.shape
    near = ref[i - 1] + ref[i + 1]
    far = ref[i - 2] + ref[i + 2]
    near += pltpu.roll(w, 1, 1) + pltpu.roll(w, depth - 1, 1)
    far += pltpu.roll(w, 2, 1) + pltpu.roll(w, depth - 2, 1)
    near += pltpu.roll(w, 1, 0) + pltpu.roll(w, rows - 1, 0)
    far += pltpu.roll(w, 2, 0) + pltpu.roll(w, rows - 2, 0)
    return -7.5 * w + NEAR * near + FAR * far


def first_rows(shape):
    return lax.broadcasted_iota(jnp.int32, shape, 0) < TILE // 2


def offsets(widths, change):
    return [sum(w + change for w in widths[:k]) for k in range(len(widths))]


def widen(out, k, widths, centre, halos):
    yl, yh, xla, xha, xlb, xhb = halos
    planes, half, depth = centre.shape
    width = widths[k]
    y_at, c_at = y_offsets(widths, planes)
    y_at, c_at = y_at[k], c_at[k]
    a_at, b_at = offsets(widths, -2)[k], offsets(widths, 2)[k]
    upper = first_rows((TILE, depth))
    none = jnp.zeros((TILE, depth), jnp.float32)
    for i in range(planes):
        for y, rows in ((yl, slice(0, TILE)), (yh, slice(TILE + half, None))):
            if width == WIDE:
                tile = y[y_at + i]
            elif i < planes // 2:
                tile = y[y_at + i]
            else:
                tile = pltpu.roll(y[y_at + i - planes // 2], TILE // 2, 0)
            out[width + i, rows, :] = tile
        out[width + i, TILE : TILE + half, :] = centre[i]
    for i in range(width):
        for low in (True, False):
            xa, xb = (xla, xlb) if low else (xha, xhb)
            j = i - 2 if low else i
            to = i if low else width + planes + i
            if 0 <= j < width - 2:
                a = xa[a_at + j]
                below, above = yl[c_at + j], yh[c_at + j]
                if not low:
                    below, above = pltpu.roll(below, TILE // 2, 0), pltpu.roll(above, TILE // 2, 0)
            else:
                a = xb[b_at + width + (i if low else j - (width - 2))]
                below = above = none
            b = xb[b_at + i]
            out[to, 0:TILE, :] = below
            out[to, TILE : 2 * TILE, :] = jnp.where(upper, a, b)
            out[to, 2 * TILE : 3 * TILE, :] = jnp.where(upper, b, a)
            out[to, 3 * TILE :, :] = above


def pack_x(fields, widths, sends):
    a_up, a_down, b_up, b_down = sends
    for k, (f, width) in enumerate(zip(fields, widths)):
        planes, _, depth = f.shape
        upper = first_rows((TILE, depth))
        a_at, b_at = offsets(widths, -2)[k], offsets(widths, 2)[k]
        for i in range(width):
            for up in (True, False):
                plane = planes - width + i if up else i
                xa, xb = (a_up, b_up) if up else (a_down, b_down)
                j = i - 2 if up else i
                first, last = f[plane, 0:TILE, :], f[plane, TILE:, :]
                a = jnp.where(upper, first, last)
                if 0 <= j < width - 2:
                    xa[a_at + j] = a
                else:
                    xb[b_at + width + (i if up else j - (width - 2))] = a
                xb[b_at + i] = jnp.where(upper, last, first)


def y_offsets(widths, planes):
    own, at = [], 0
    for width in widths:
        own.append(at)
        at += planes if width == WIDE else planes // 2
    corners = [at + c for c in offsets(widths, -2)]
    return own, corners


def y_length(widths, planes):
    return y_offsets(widths, planes)[1][-1] + widths[-1] - 2


def pack_y(widths, *refs):
    count = len(widths)
    fields, (xla, xha, y_up, y_down) = refs[:count], refs[count:]
    planes, _, depth = fields[0].shape
    own, corners = y_offsets(widths, planes)
    upper = first_rows((TILE, depth))

    def pair(at, last, first, last_turned, first_turned):
        y_up[at] = jnp.where(upper, pltpu.roll(last_turned, TILE // 2, 0), last)
        y_down[at] = jnp.where(upper, first, pltpu.roll(first_turned, TILE // 2, 0))

    for k, (f, width) in enumerate(zip(fields, widths)):
        if width == WIDE:
            y_up[pl.ds(own[k], planes)] = f[:, TILE:, :]
            y_down[pl.ds(own[k], planes)] = f[:, 0:TILE, :]
        else:
            for i in range(planes // 2):
                g = f.at[i + planes // 2]
                pair(own[k] + i, f[i, TILE:, :], f[i, 0:TILE, :], g[TILE:, :], g[0:TILE, :])
        for i in range(width - 2):
            low, high = xla[offsets(widths, -2)[k] + i], xha[offsets(widths, -2)[k] + i]
            pair(corners[k] + i, low, low, high, high)


def load_first(h, u, v, s, u_own, v_own, s_own, *rest):
    sends, sems = rest[:4], rest[4]
    half = u_own.shape[1]
    own = pl.ds(pl.multiple_of(h[0] * half, TILE), half)
    fields = (u_own, v_own, s_own)
    copies = [
        pltpu.make_async_copy(f.at[:, own, :], to, sems.at[k])
        for k, (f, to) in enumerate(zip((u, v, s), fields))
    ]
    for copy in copies:
        copy.start()
    for copy in copies:
        copy.wait()
    pack_x(fields, FIRST, sends)


def own_rows(i, count):
    return slice(TILE, 3 * TILE) if i < 2 or i >= count - 2 else slice(0, 4 * TILE)


def first_step(planes, v0, q0, s, v1, q1):
    count = planes + 2 * MID
    for i in range(count):
        rows = own_rows(i, count)
        l = lap(v0, i + 2)[rows]
        v1[i, rows, :] = v0[i + 2, rows, :] + time_step * (s[i, rows, :] * q0[i, rows, :] + damping * l)
        if 2 <= i < count - 2:
            q1[i - 2] = q0[i] + time_step * l


def two_steps(planes, v0, q0, s, v1, q1, v2, q2):
    first_step(planes, v0, q0, s, v1, q1)
    count = planes + 4
    own = slice(TILE, 3 * TILE)
    for i in range(count):
        rows = own_rows(i, count)
        l = lap(v1, i + 2)
        rate = s[i + 2, rows, :] * q1[i, rows, :] + damping * l[rows]
        v2[i, rows, :] = v1[i + 2, rows, :] + time_step * rate
        if 2 <= i < count - 2:
            q2[i - 2] = q1[i, own, :] + time_step * l[own]


def third_step(planes, u, v0, v1, v2, q2, s, u_out, v_out, q_out):
    own = slice(TILE, 3 * TILE)
    for i in range(planes):
        l = lap(v2, i + 2)[own]
        v_out[i] = v2[i + 2, own, :] + time_step * (s[i + MID, own, :] * q2[i] + damping * l)
        q_out[i] = q2[i] + time_step * l
        moved = v0[i + WIDE, own, :] + v1[i + MID, own, :] + v2[i + 2, own, :]
        u_out[i] = u[i] + time_step * moved


def first_steps(u, v, s, *rest):
    halos, (u_out, v_out, q_out, s_wide), sends = rest[:6], rest[6:10], rest[10:14]
    u0, v0, q0, v1, q1, v2, q2 = rest[14:]
    planes, _, _ = u.shape
    for k, (f, out) in enumerate(((u, u0), (v, v0), (s, s_wide))):
        widen(out, k, FIRST, f, halos)
    count = planes + 2 * MID
    for i in range(count):
        rows = own_rows(i, count)
        q0[i, rows, :] = lap(u0, i + 2)[rows]
    two_steps(planes, v0, q0, s_wide, v1, q1, v2, q2)
    third_step(planes, u, v0, v1, v2, q2, s_wide, u_out, v_out, q_out)
    pack_x((v_out, q_out), LATER, sends)


def middle_steps(u, v, q, s_wide, *rest):
    halos, (u_out, v_out, q_out), sends = rest[:6], rest[6:9], rest[9:13]
    v0, q0, v1, q1, v2, q2 = rest[13:]
    planes, _, _ = v.shape
    widen(v0, 0, LATER, v, halos)
    widen(q0, 1, LATER, q, halos)
    two_steps(planes, v0, q0, s_wide, v1, q1, v2, q2)
    third_step(planes, u, v0, v1, v2, q2, s_wide, u_out, v_out, q_out)
    pack_x((v_out, q_out), LATER, sends)


def last_steps(scale, u, v, q, s_wide, *rest):
    halos, (keep, send), (v0, q0, v1, q1, rate, l7) = rest[:6], rest[6:8], rest[8:]
    planes, _, _ = v.shape
    own = slice(TILE, 3 * TILE)
    widen(v0, 0, LATER, v, halos)
    widen(q0, 1, LATER, q, halos)
    first_step(planes, v0, q0, s_wide, v1, q1)
    count = planes + 4
    for i in range(count):
        rows = own_rows(i, count)
        l = lap(v1, i + 2)
        rate[i, rows, :] = s_wide[i + 2, rows, :] * q1[i, rows, :] + damping * l[rows]
        if 2 <= i < count - 2:
            l7[i - 2] = l[own]
    for i in range(planes):
        l = lap(rate, i + 2)[own]
        r = rate[i + 2, own, :]
        u8 = u[i] + time_step * (v[i] + v1[i + MID, own, :])
        v8 = v1[i + MID, own, :] + time_step * r
        more = s_wide[i + MID, own, :] * l7[i] + damping * l
        keep[i] = u8 + scale[0] * r
        keep[planes + i] = v8 + scale[0] * more
        send[i] = u8 + scale[1] * r
        send[planes + i] = v8 + scale[1] * more


def join(h, keep, got, out_u, out_v):
    planes, rows, _ = out_u.shape
    half = rows // 2
    own = pl.ds(pl.multiple_of(h[0] * half, TILE), half)
    other = pl.ds(pl.multiple_of((1 - h[0]) * half, TILE), half)
    for k, out in enumerate((out_u, out_v)):
        part = pl.ds(k * planes, planes)
        out[:, own, :] = keep[part]
        out[:, other, :] = got[part]


def ring(count, step):
    return [(i, (i + step) % count) for i in range(count)]


def strips(gy, step):
    def place(t):
        j, h = divmod(t % (2 * gy), 2)
        return ((h + j) % 2) * gy + j

    return [(place(t), place(t + step)) for t in range(2 * gy)]


STARTS = ("a_up", "a_down", "b_up", "b_down", "y_up", "y_down")


def exchange(fields, widths, sends):
    gx, gy = lax.axis_size("gx"), lax.axis_size("gy")
    planes, _, depth = fields[0].shape
    got = {}

    def move(name, sent, axis, pairs):
        got[name] = lax.ppermute(sent, axis, pairs)

    for name, sent in zip(STARTS, sends):
        move(name, sent, "gx", ring(gx, 1 if name.endswith("up") else -1))
    y = spec(y_length(widths, planes), TILE, depth)
    args = (*fields, got["a_up"], got["a_down"])
    y_up, y_down = call(functools.partial(pack_y, widths), [y, y], args)
    move("y_up", y_up, ("level", "gy"), strips(gy, 1))
    move("y_down", y_down, ("level", "gy"), strips(gy, -1))
    return [got[name] for name in ("y_up", "y_down", "a_up", "a_down", "b_up", "b_down")]


def edge_specs(depth, widths):
    counts = sum(w - 2 for w in widths), sum(w + 2 for w in widths)
    return [spec(count, TILE, depth) for count in counts for _ in range(2)]


def body(u, v, s):
    planes, rows, depth = u.shape
    half = rows // 2
    assert lax.axis_size("level") == 2 and planes >= WIDE and half == 2 * TILE
    level = lax.axis_index("level")
    h = ((level + lax.axis_index("gy")) % 2).astype(jnp.int32).reshape(1)
    mine = jnp.where(level == 0, 0.0, second).astype(jnp.float32)
    scale = jnp.stack([mine, second - mine])

    tall = half + 2 * TILE
    block = spec(planes, half, depth)
    wide = (planes + 2 * WIDE, tall, depth)
    mid = (planes + 2 * MID, tall, depth)
    thin = (planes + 4, tall, depth)
    bare = (planes, half, depth)
    work = 100 * u.size
    sent = edge_specs(depth, LATER)

    outs = [block] * 3 + edge_specs(depth, FIRST)
    u, v, s, *sends = pl.pallas_call(
        load_first,
        out_shape=outs,
        in_specs=[SMEM] + [pl.BlockSpec(memory_space=pltpu.HBM)] * 3,
        out_specs=[VMEM] * len(outs),
        scratch_shapes=[pltpu.SemaphoreType.DMA((3,))],
        compiler_params=pltpu.CompilerParams(vmem_limit_bytes=10 << 20),
    )(h, *(pltpu.with_memory_space_constraint(f, pltpu.HBM) for f in (u, v, s)))
    halos = exchange((u, v, s), FIRST, sends)
    u, v, q, s_wide, *sends = call(
        first_steps,
        [block] * 3 + [spec(*mid)] + sent,
        (u, v, s, *halos),
        (),
        (wide, wide, mid, mid, thin, thin, bare),
        work,
    )
    halos = exchange((v, q), LATER, sends)
    u, v, q, *sends = call(
        middle_steps,
        [block] * 3 + sent,
        (u, v, q, s_wide, *halos),
        (),
        (wide, mid, mid, thin, thin, bare),
        work,
    )
    halos = exchange((v, q), LATER, sends)
    both = spec(2 * planes, half, depth)
    keep, send = call(
        last_steps,
        [both, both],
        (u, v, q, s_wide, *halos),
        (scale,),
        (wide, mid, mid, thin, thin, (planes, half, depth)),
        work,
    )
    got = lax.ppermute(send, "level", ring(2, 1))
    out_u, out_v = call(join, [spec(planes, rows, depth)] * 2, (keep, got), (h,))
    return out_u[None], out_v[None]


def solution(mesh):
    placed = (P("gx", "gy", None),) * 3
    return jax.shard_map(
        body,
        mesh=mesh,
        in_specs=placed,
        out_specs=(P("level", "gx", "gy", None), P("level", "gx", "gy", None)),
        check_vma=False,
    )
```

```python
import functools

import jax
import jax.numpy as jnp
from jax import lax
from jax.experimental import pallas as pl
from jax.experimental.pallas import tpu as pltpu
from jax.sharding import PartitionSpec as P


STEPS = 8

time_step = 0.12
damping = 0.05
second = 0.5 * STEPS * time_step * time_step

NEAR = 4.0 / 3.0
FAR = -1.0 / 12.0

TILE = 8
WIDE = 8
MID = 6
LATER = (WIDE, MID)

VMEM = pl.BlockSpec(memory_space=pltpu.VMEM)
SMEM = pl.BlockSpec(memory_space=pltpu.SMEM)
OWN = slice(TILE, 3 * TILE)
ALL = slice(0, 4 * TILE)


def spec(*shape):
    return jax.ShapeDtypeStruct(shape, jnp.float32)


def call(kernel, outs, args, scalars=(), scratch=(), flops=0):
    moved = 4 * (sum(a.size for a in args) + sum(o.size for o in outs))
    return pl.pallas_call(
        kernel,
        out_shape=outs,
        in_specs=[SMEM] * len(scalars) + [VMEM] * len(args),
        out_specs=[VMEM] * len(outs),
        scratch_shapes=[pltpu.VMEM(shape, jnp.float32) for shape in scratch],
        compiler_params=pltpu.CompilerParams(vmem_limit_bytes=14 << 20),
        cost_estimate=pl.CostEstimate(flops=flops, bytes_accessed=moved, transcendentals=0),
    )(*scalars, *args)


def upper():
    return lax.broadcasted_iota(jnp.int32, (TILE, 1), 0) < TILE // 2


def turned(tile):
    return pltpu.roll(tile, TILE // 2, 0)


def lap(ref, i, rows):
    full = ref[i]
    count, depth = full.shape
    w = full[rows]
    near = ref[i - 1, rows, :] + ref[i + 1, rows, :]
    far = ref[i - 2, rows, :] + ref[i + 2, rows, :]
    near += pltpu.roll(w, 1, 1) + pltpu.roll(w, depth - 1, 1)
    far += pltpu.roll(w, 2, 1) + pltpu.roll(w, depth - 2, 1)
    near += pltpu.roll(full, 1, 0)[rows] + pltpu.roll(full, count - 1, 0)[rows]
    far += pltpu.roll(full, 2, 0)[rows] + pltpu.roll(full, count - 2, 0)[rows]
    return -7.5 * w + NEAR * near + FAR * far


def beyond(width, d):
    return max(0, width - 2 * ((d + 1) // 2))


def x_layout(widths):
    first, rest = {}, {}
    for k, width in enumerate(widths):
        for d in range(1, width + 1):
            for part, least in (("A", 0), ("B", TILE // 2)):
                into = first if beyond(width, d) > least else rest
                into[k, d, part] = len(into)
    return first, rest


def y_layout(planes, widths, corners):
    at = len(widths) * planes
    where = {}
    for k, width in enumerate(corners):
        for d in range(1, width + 1):
            rows = beyond(width, d)
            if rows > 0:
                where[k, d] = at
                at += 2 if rows > TILE // 2 else 1
    return where, at


def pack_x(fields, widths, sends):
    a_up, a_down, b_up, b_down = sends
    first, rest = x_layout(widths)
    for k, (f, width) in enumerate(zip(fields, widths)):
        planes = f.shape[0]
        for d in range(1, width + 1):
            for plane, xa, xb in ((planes - d, a_up, b_up), (d - 1, a_down, b_down)):
                low, high = f[plane, 0:TILE, :], f[plane, TILE:, :]
                for part, tile in (
                    ("A", jnp.where(upper(), low, high)),
                    ("B", jnp.where(upper(), high, low)),
                ):
                    if (k, d, part) in first:
                        xa[first[k, d, part]] = tile
                    else:
                        xb[rest[k, d, part]] = tile


def pack_y(extra, *refs):
    planes = refs[0].shape[0]
    v, q, xla, xha = refs[:4]
    y_up, y_down = refs[-2:]
    corners = LATER + ((MID,) if extra else ())
    where, _ = y_layout(planes, LATER, corners)
    first, _ = x_layout(LATER)
    for k, f in enumerate((v, q)):
        y_up[pl.ds(k * planes, planes)] = f[:, TILE:, :]
        y_down[pl.ds(k * planes, planes)] = f[:, 0:TILE, :]
    for (k, d), at in where.items():
        if k == 2:
            low, high = refs[4], refs[5]
            i, j = 4 + MID - d, 4 + d - 1
            a_low = jnp.where(upper(), low[i, 0:TILE, :], low[i, TILE:, :])
            a_high = jnp.where(upper(), high[j, 0:TILE, :], high[j, TILE:, :])
        else:
            a_low, a_high = xla[first[k, d, "A"]], xha[first[k, d, "A"]]
        if beyond(corners[k], d) > TILE // 2:
            for side, a, x in ((0, a_low, xla), (1, a_high, xha)):
                b = x[first[k, d, "B"]]
                y_up[at + side] = jnp.where(upper(), b, a)
                y_down[at + side] = jnp.where(upper(), a, b)
        else:
            y_up[at] = jnp.where(upper(), turned(a_high), a_low)
            y_down[at] = jnp.where(upper(), a_low, turned(a_high))


def widen(out, width, centre, y_tile, x_tiles, corner):
    planes, _, depth = centre.shape
    for i in range(planes):
        out[width + i, 0:TILE, :] = y_tile(0, i)
        out[width + i, OWN, :] = centre[i]
        out[width + i, 3 * TILE :, :] = y_tile(1, i)
    for d in range(1, width + 1):
        for side, to in ((0, width - d), (1, width + planes - 1 + d)):
            low, high = x_tiles(side, d)
            out[to, TILE : 2 * TILE, :] = low
            out[to, 2 * TILE : 3 * TILE, :] = high
            if beyond(width, d) > 0:
                out[to, 0:TILE, :] = corner(side, 0, d)
                out[to, 3 * TILE :, :] = corner(side, 1, d)
            else:
                out[to, 0:TILE, :] = jnp.zeros((TILE, depth), jnp.float32)
                out[to, 3 * TILE :, :] = jnp.zeros((TILE, depth), jnp.float32)


def corner_of(k, corners, where, y):
    def corner(side, y_side, d):
        at = where[k, d]
        if beyond(corners[k], d) > TILE // 2:
            return y[y_side][at + side]
        tile = y[y_side][at]
        return turned(tile) if side else tile

    return corner


def widen_moved(outs, fields, corners, y, xa, xb):
    planes = fields[0].shape[0]
    where, _ = y_layout(planes, LATER, corners)
    first, rest = x_layout(LATER)
    for k, (out, f) in enumerate(zip(outs, fields)):

        def tile(side, d, part):
            key = k, d, part
            return xa[side][first[key]] if key in first else xb[side][rest[key]]

        def x_tiles(side, d):
            a, b = tile(side, d, "A"), tile(side, d, "B")
            return jnp.where(upper(), a, b), jnp.where(upper(), b, a)

        widen(
            out,
            LATER[k],
            f,
            lambda side, i: y[side][k * planes + i],
            x_tiles,
            corner_of(k, corners, where, y),
        )


def load_first(h, u, v, s, u_own, v_own, s_own, y_up, y_down, x_up, x_down, sems):
    planes, half, _ = u_own.shape
    own = pl.ds(pl.multiple_of(h[0] * half, TILE), half)
    fields = (u_own, v_own, s_own)
    copies = [
        pltpu.make_async_copy(f.at[:, own, :], to, sems.at[k])
        for k, (f, to) in enumerate(zip((u, v, s), fields))
    ]
    for copy in copies:
        copy.start()
    for copy in copies:
        copy.wait()
    at = 0
    for k, (f, width) in enumerate(zip(fields, (2, 2, MID))):
        x_up[pl.ds(at, width)] = f[planes - width :]
        x_down[pl.ds(at, width)] = f[0:width]
        y_up[pl.ds(k * planes, planes)] = f[:, TILE:, :]
        y_down[pl.ds(k * planes, planes)] = f[:, 0:TILE, :]
        at += width


def first_step(u, v, s, yl, yh, xl, xh, u_out, v_out, q_out, *rest):
    sends, (u0, v0) = rest[:4], rest[4:]
    planes, _, _ = u.shape
    for k, (f, out) in enumerate(((u, u0), (v, v0))):
        inner = pl.ds(2, planes)
        out[inner, 0:TILE, :] = yl[pl.ds(k * planes, planes)]
        out[inner, OWN, :] = f[...]
        out[inner, 3 * TILE :, :] = yh[pl.ds(k * planes, planes)]
        out[0:2, OWN, :] = xl[pl.ds(2 * k, 2)]
        out[planes + 2 :, OWN, :] = xh[pl.ds(2 * k, 2)]
    for i in range(planes):
        q, l = lap(u0, i + 2, OWN), lap(v0, i + 2, OWN)
        u_out[i] = u[i] + time_step * v[i]
        v_out[i] = v[i] + time_step * (s[i] * q + damping * l)
        q_out[i] = q + time_step * l
    pack_x((v_out, q_out), LATER, sends)


def advance(planes, width, v, q, s, v_out, q_out):
    count = planes + 2 * width - 4
    for i in range(count):
        edge = i < 2 or i >= count - 2
        rows = OWN if edge else ALL
        l = lap(v, i + 2, rows)
        now = s[i + MID + 2 - width, rows, :] * q[i, rows, :] + damping * l
        v_out[i, rows, :] = v[i + 2, rows, :] + time_step * now
        if not edge:
            q_out[i - 2] = q[i] + time_step * l


def middle_steps(u, v, q, s, yl, yh, xla, xha, xlb, xhb, ysl, ysh, xsl, xsh, *rest):
    (u_out, v_out, q_out, s_wide), sends = rest[:4], rest[4:8]
    v0, q0, v1, q1, v2, q2, v3, q3 = rest[8:]
    planes, _, _ = v.shape
    corners = LATER + (MID,)
    where, _ = y_layout(planes, LATER, corners)

    def s_rows(side, d):
        ref, i = ((xsl, 4 + MID - d), (xsh, 4 + d - 1))[side]
        return ref[i, 0:TILE, :], ref[i, TILE:, :]

    widen_moved((v0, q0), (v, q), corners, (yl, yh), (xla, xha), (xlb, xhb))
    widen(
        s_wide,
        MID,
        s,
        lambda side, i: (ysl, ysh)[side][2 * planes + i],
        s_rows,
        corner_of(2, corners, where, (yl, yh)),
    )
    advance(planes, WIDE, v0, q0, s_wide, v1, q1)
    advance(planes, WIDE - 2, v1, q1, s_wide, v2, q2)
    advance(planes, WIDE - 4, v2, q2, s_wide, v3, q3)
    for i in range(planes):
        l = lap(v3, i + 2, OWN)
        now = s[i] * q3[i, OWN, :] + damping * l
        v_out[i] = v3[i + 2, OWN, :] + time_step * now
        q_out[i] = q3[i, OWN, :] + time_step * l
        moved = v[i] + v1[i + 6, OWN, :] + v2[i + 4, OWN, :] + v3[i + 2, OWN, :]
        u_out[i] = u[i] + time_step * moved
    pack_x((v_out, q_out), LATER, sends)


def last_steps(scale, u, v, q, s_wide, yl, yh, xla, xha, xlb, xhb, keep, send, *scratch):
    v0, q0, v1, q1, v2, q2, rate, l7 = scratch
    planes, _, _ = v.shape
    widen_moved((v0, q0), (v, q), LATER, (yl, yh), (xla, xha), (xlb, xhb))
    advance(planes, WIDE, v0, q0, s_wide, v1, q1)
    advance(planes, WIDE - 2, v1, q1, s_wide, v2, q2)
    count = planes + 4
    for i in range(count):
        edge = i < 2 or i >= count - 2
        rows = OWN if edge else ALL
        l = lap(v2, i + 2, rows)
        rate[i, rows, :] = s_wide[i + MID - 2, rows, :] * q2[i, rows, :] + damping * l
        if not edge:
            l7[i - 2] = l[OWN]
    for i in range(planes):
        l = lap(rate, i + 2, OWN)
        r = rate[i + 2, OWN, :]
        v7 = v2[i + 4, OWN, :]
        u8 = u[i] + time_step * (v[i] + v1[i + 6, OWN, :] + v7)
        v8 = v7 + time_step * r
        more = s_wide[i + MID, OWN, :] * l7[i] + damping * l
        keep[i] = u8 + scale[0] * r
        keep[planes + i] = v8 + scale[0] * more
        send[i] = u8 + scale[1] * r
        send[planes + i] = v8 + scale[1] * more


def join(h, keep, got, out_u, out_v):
    planes, rows, _ = out_u.shape
    half = rows // 2
    own = pl.ds(pl.multiple_of(h[0] * half, TILE), half)
    other = pl.ds(pl.multiple_of((1 - h[0]) * half, TILE), half)
    for k, out in enumerate((out_u, out_v)):
        part = pl.ds(k * planes, planes)
        out[:, own, :] = keep[part]
        out[:, other, :] = got[part]


def ring(count, step):
    return [(i, (i + step) % count) for i in range(count)]


def strips(gy, step):
    def place(t):
        j, h = divmod(t % (2 * gy), 2)
        return ((h + j) % 2) * gy + j

    return [(place(t), place(t + step)) for t in range(2 * gy)]


STARTS = ("a_up", "a_down", "b_up", "b_down", "y_up", "y_down")


def move(name, sent):
    step = 1 if name.endswith("up") else -1
    if name.startswith("y"):
        return lax.ppermute(sent, ("level", "gy"), strips(lax.axis_size("gy"), step))
    return lax.ppermute(sent, "gx", ring(lax.axis_size("gx"), step))


def exchange_first(y_up, y_down, x_up, x_down):
    xl, xh = move("a_up", x_up), move("a_down", x_down)
    return move("y_up", y_up), move("y_down", y_down), xl, xh


def exchange(v, q, sends, extra):
    planes, _, depth = v.shape
    xla, xha, xlb, xhb = (move(name, sent) for name, sent in zip(STARTS, sends))
    corners = LATER + ((MID,) if extra else ())
    y = spec(y_layout(planes, LATER, corners)[1], TILE, depth)
    kernel = functools.partial(pack_y, bool(extra))
    y_up, y_down = call(kernel, [y, y], (v, q, xla, xha, *extra))
    return move("y_up", y_up), move("y_down", y_down), xla, xha, xlb, xhb


def edge_specs(depth, widths):
    return [spec(len(part), TILE, depth) for part in x_layout(widths) for _ in range(2)]


def body(u, v, s):
    planes, rows, depth = u.shape
    half = rows // 2
    assert lax.axis_size("level") == 2 and planes >= WIDE and half == 2 * TILE
    level = lax.axis_index("level")
    h = ((level + lax.axis_index("gy")) % 2).astype(jnp.int32).reshape(1)
    mine = jnp.where(level == 0, 0.0, second).astype(jnp.float32)
    scale = jnp.stack([mine, second - mine])

    tall = half + 2 * TILE
    block = spec(planes, half, depth)
    wide, mid, thin, slim, bare = ((planes + 2 * w, tall, depth) for w in (WIDE, MID, 4, 2, 0))
    work = 100 * u.size
    sent = edge_specs(depth, LATER)

    y, x = spec(3 * planes, TILE, depth), spec(4 + MID, half, depth)
    outs = [block] * 3 + [y, y, x, x]
    u, v, s, *sends = pl.pallas_call(
        load_first,
        out_shape=outs,
        in_specs=[SMEM] + [pl.BlockSpec(memory_space=pltpu.HBM)] * 3,
        out_specs=[VMEM] * len(outs),
        scratch_shapes=[pltpu.SemaphoreType.DMA((3,))],
        compiler_params=pltpu.CompilerParams(vmem_limit_bytes=14 << 20),
    )(h, *(pltpu.with_memory_space_constraint(f, pltpu.HBM) for f in (u, v, s)))
    halos = exchange_first(*sends)
    ysl, ysh, xsl, xsh = halos
    args = (u, v, s, *halos)
    u, v, q, *sends = call(first_step, [block] * 3 + sent, args, (), (slim, slim), work)
    halos = exchange(v, q, sends, (xsl, xsh))
    u, v, q, s_wide, *sends = call(
        middle_steps,
        [block] * 3 + [spec(*mid)] + sent,
        (u, v, q, s, *halos, ysl, ysh, xsl, xsh),
        (),
        (wide, mid, mid, thin, thin, slim, slim, bare),
        work,
    )
    halos = exchange(v, q, sends, ())
    both = spec(2 * planes, half, depth)
    keep, send = call(
        last_steps,
        [both, both],
        (u, v, q, s_wide, *halos),
        (scale,),
        (wide, mid, mid, thin, thin, slim, slim, (planes, half, depth)),
        work,
    )
    got = lax.ppermute(send, "level", ring(2, 1))
    out_u, out_v = call(join, [spec(planes, rows, depth)] * 2, (keep, got), (h,))
    return out_u[None], out_v[None]


def solution(mesh):
    placed = (P("gx", "gy", None),) * 3
    return jax.shard_map(
        body,
        mesh=mesh,
        in_specs=placed,
        out_specs=(P("level", "gx", "gy", None), P("level", "gx", "gy", None)),
        check_vma=False,
    )
```

```python
import jax
import jax.numpy as jnp
from jax import lax
from jax.experimental import pallas as pl
from jax.experimental.pallas import tpu as pltpu
from jax.sharding import PartitionSpec as P


STEPS = 8

time_step = 0.12
damping = 0.05
second = 0.5 * STEPS * time_step * time_step

NEAR = 4.0 / 3.0
FAR = -1.0 / 12.0

TILE = 8
WIDE = 8
MID = 6
LATER = (WIDE, MID)

VMEM = pl.BlockSpec(memory_space=pltpu.VMEM)
SMEM = pl.BlockSpec(memory_space=pltpu.SMEM)
OWN = slice(TILE, 3 * TILE)
ALL = slice(0, 4 * TILE)


def spec(*shape):
    return jax.ShapeDtypeStruct(shape, jnp.float32)


def call(kernel, outs, args, scalars=(), scratch=(), flops=0):
    moved = 4 * (sum(a.size for a in args) + sum(o.size for o in outs))
    return pl.pallas_call(
        kernel,
        out_shape=outs,
        in_specs=[SMEM] * len(scalars) + [VMEM] * len(args),
        out_specs=[VMEM] * len(outs),
        scratch_shapes=[pltpu.VMEM(shape, jnp.float32) for shape in scratch],
        compiler_params=pltpu.CompilerParams(vmem_limit_bytes=14 << 20),
        cost_estimate=pl.CostEstimate(flops=flops, bytes_accessed=moved, transcendentals=0),
    )(*scalars, *args)


def upper():
    return lax.broadcasted_iota(jnp.int32, (TILE, 1), 0) < TILE // 2


def turned(tile):
    return pltpu.roll(tile, TILE // 2, 0)


def lap(ref, i, rows):
    full = ref[i]
    count, depth = full.shape
    w = full[rows]
    near = ref[i - 1, rows, :] + ref[i + 1, rows, :]
    far = ref[i - 2, rows, :] + ref[i + 2, rows, :]
    near += pltpu.roll(w, 1, 1) + pltpu.roll(w, depth - 1, 1)
    far += pltpu.roll(w, 2, 1) + pltpu.roll(w, depth - 2, 1)
    near += pltpu.roll(full, 1, 0)[rows] + pltpu.roll(full, count - 1, 0)[rows]
    far += pltpu.roll(full, 2, 0)[rows] + pltpu.roll(full, count - 2, 0)[rows]
    return -7.5 * w + NEAR * near + FAR * far


def beyond(width, d):
    return max(0, width - 2 * ((d + 1) // 2))


def x_layout(widths):
    first, rest = {}, {}
    for k, width in enumerate(widths):
        for d in range(1, width + 1):
            for part, least in (("A", 0), ("B", TILE // 2)):
                into = first if beyond(width, d) > least else rest
                into[k, d, part] = len(into)
    return first, rest


def corner_layout(widths, at=0):
    where = {}
    for k, width in enumerate(widths):
        for d in range(1, width + 1):
            rows = beyond(width, d)
            if rows > 0:
                where[k, d] = at
                at += 2 if rows > TILE // 2 else 1
    return where, at


def pack_x(fields, widths, sends):
    a_up, a_down, b_up, b_down = sends
    first, rest = x_layout(widths)
    for k, (f, width) in enumerate(zip(fields, widths)):
        planes = f.shape[0]
        for d in range(1, width + 1):
            for plane, xa, xb in ((planes - d, a_up, b_up), (d - 1, a_down, b_down)):
                low, high = f[plane, 0:TILE, :], f[plane, TILE:, :]
                for part, tile in (
                    ("A", jnp.where(upper(), low, high)),
                    ("B", jnp.where(upper(), high, low)),
                ):
                    if (k, d, part) in first:
                        xa[first[k, d, part]] = tile
                    else:
                        xb[rest[k, d, part]] = tile


def put_shared(at, a_low, a_high, y_up, y_down):
    y_up[at] = jnp.where(upper(), turned(a_high), a_low)
    y_down[at] = jnp.where(upper(), a_low, turned(a_high))


def pack_rows(*refs):
    (v, q, *extra), (y_up, y_down) = refs[:-2], refs[-2:]
    planes = v.shape[0]
    for k, f in enumerate((v, q)):
        y_up[pl.ds(k * planes, planes)] = f[:, TILE:, :]
        y_down[pl.ds(k * planes, planes)] = f[:, 0:TILE, :]
    if extra:
        for (_, d), at in corner_layout((MID,), 2 * planes)[0].items():
            low, high = extra[0].at[MID - d], extra[1].at[d - 1]
            a_low = jnp.where(upper(), low[0:TILE, :], low[TILE:, :])
            a_high = jnp.where(upper(), high[0:TILE, :], high[TILE:, :])
            put_shared(at, a_low, a_high, y_up, y_down)


def pack_corners(xla, xha, c_up, c_down):
    first, _ = x_layout(LATER)
    for (k, d), at in corner_layout(LATER)[0].items():
        if beyond(LATER[k], d) > TILE // 2:
            for side, x in ((0, xla), (1, xha)):
                a, b = x[first[k, d, "A"]], x[first[k, d, "B"]]
                c_up[at + side] = jnp.where(upper(), b, a)
                c_down[at + side] = jnp.where(upper(), a, b)
        else:
            put_shared(at, xla[first[k, d, "A"]], xha[first[k, d, "A"]], c_up, c_down)


def widen(out, width, centre, y_tile, x_tiles, corner):
    planes, _, depth = centre.shape
    for i in range(planes):
        out[width + i, 0:TILE, :] = y_tile(0, i)
        out[width + i, OWN, :] = centre[i]
        out[width + i, 3 * TILE :, :] = y_tile(1, i)
    for d in range(1, width + 1):
        for side, to in ((0, width - d), (1, width + planes - 1 + d)):
            low, high = x_tiles(side, d)
            out[to, TILE : 2 * TILE, :] = low
            out[to, 2 * TILE : 3 * TILE, :] = high
            if beyond(width, d) > 0:
                out[to, 0:TILE, :] = corner(side, 0, d)
                out[to, 3 * TILE :, :] = corner(side, 1, d)
            else:
                out[to, 0:TILE, :] = jnp.zeros((TILE, depth), jnp.float32)
                out[to, 3 * TILE :, :] = jnp.zeros((TILE, depth), jnp.float32)


def corner_of(k, widths, where, c):
    def corner(side, y_side, d):
        at = where[k, d]
        if beyond(widths[k], d) > TILE // 2:
            return c[y_side][at + side]
        tile = c[y_side][at]
        return turned(tile) if side else tile

    return corner


def widen_moved(outs, fields, halos):
    y, xa, xb, c = (halos[i : i + 2] for i in range(0, 8, 2))
    planes = fields[0].shape[0]
    where, _ = corner_layout(LATER)
    first, rest = x_layout(LATER)
    for k, (out, f) in enumerate(zip(outs, fields)):

        def tile(side, d, part):
            key = k, d, part
            return xa[side][first[key]] if key in first else xb[side][rest[key]]

        def x_tiles(side, d):
            a, b = tile(side, d, "A"), tile(side, d, "B")
            return jnp.where(upper(), a, b), jnp.where(upper(), b, a)

        widen(
            out,
            LATER[k],
            f,
            lambda side, i: y[side][k * planes + i],
            x_tiles,
            corner_of(k, LATER, where, c),
        )


def load_first(h, u, v, s, u_own, v_own, s_own, *rest):
    x_up, x_down, y_up, y_down, s_up, s_down, sems = rest
    planes, half, _ = u_own.shape
    own = pl.ds(pl.multiple_of(h[0] * half, TILE), half)
    fields = (u_own, v_own, s_own)
    copies = [
        pltpu.make_async_copy(f.at[:, own, :], to, sems.at[k])
        for k, (f, to) in enumerate(zip((u, v, s), fields))
    ]
    for copy in copies:
        copy.start()
    for copy in copies:
        copy.wait()
    for k, f in enumerate((u_own, v_own)):
        x_up[pl.ds(2 * k, 2)] = f[planes - 2 :]
        x_down[pl.ds(2 * k, 2)] = f[0:2]
    s_up[...] = s_own[planes - MID :]
    s_down[...] = s_own[0:MID]
    pairs = planes // 2
    group = lax.broadcasted_iota(jnp.int32, (TILE, 1), 0) // 2
    for i in range(pairs):
        shared = (u_own, i), (v_own, i), (u_own, i + pairs), (v_own, i + pairs)
        top = bottom = None
        for n, (f, plane) in enumerate(shared):
            last, first = f[plane, TILE:, :], f[plane, 0:TILE, :]
            if n == 0:
                top, bottom = last, first
            else:
                top = jnp.where(group == 3 - n, pltpu.roll(last, TILE - 2 * n, 0), top)
                bottom = jnp.where(group == n, pltpu.roll(first, 2 * n, 0), bottom)
        y_up[i] = top
        y_down[i] = bottom
    y_up[pairs:] = s_own[:, TILE:, :]
    y_down[pairs:] = s_own[:, 0:TILE, :]


def first_step(u, v, s, yl, yh, xl, xh, u_out, v_out, q_out, *rest):
    sends, (u0, v0) = rest[:4], rest[4:]
    planes, _, _ = u.shape
    pairs = planes // 2
    for k, (f, out) in enumerate(((u, u0), (v, v0))):
        out[pl.ds(2, planes), OWN, :] = f[...]
        out[0:2, OWN, :] = xl[pl.ds(2 * k, 2)]
        out[planes + 2 :, OWN, :] = xh[pl.ds(2 * k, 2)]
        for i in range(planes):
            n = k + 2 * (i // pairs)
            below, above = yl[i % pairs], yh[i % pairs]
            if n > 0:
                below, above = pltpu.roll(below, 2 * n, 0), pltpu.roll(above, TILE - 2 * n, 0)
            out[2 + i, 0:TILE, :] = below
            out[2 + i, 3 * TILE :, :] = above
    for i in range(planes):
        q, l = lap(u0, i + 2, OWN), lap(v0, i + 2, OWN)
        u_out[i] = u[i] + time_step * v[i]
        v_out[i] = v[i] + time_step * (s[i] * q + damping * l)
        q_out[i] = q + time_step * l
    pack_x((v_out, q_out), LATER, sends)


def advance(planes, width, v, q, s, v_out, q_out):
    count = planes + 2 * width - 4
    for i in range(count):
        edge = i < 2 or i >= count - 2
        rows = OWN if edge else ALL
        l = lap(v, i + 2, rows)
        now = s[i + MID + 2 - width, rows, :] * q[i, rows, :] + damping * l
        v_out[i, rows, :] = v[i + 2, rows, :] + time_step * now
        if not edge:
            q_out[i - 2] = q[i] + time_step * l


def middle_steps(u, v, q, s, *rest):
    halos, (ysl, ysh, xsl, xsh), rest = rest[:8], rest[8:12], rest[12:]
    (u_out, v_out, q_out, s_wide), sends = rest[:4], rest[4:8]
    v0, q0, v1, q1, v2, q2, v3, q3 = rest[8:]
    planes, _, _ = v.shape
    where, _ = corner_layout((MID,), 2 * planes)

    def s_rows(side, d):
        ref, i = ((xsl, MID - d), (xsh, d - 1))[side]
        return ref[i, 0:TILE, :], ref[i, TILE:, :]

    widen_moved((v0, q0), (v, q), halos)
    widen(
        s_wide,
        MID,
        s,
        lambda side, i: (ysl, ysh)[side][planes // 2 + i],
        s_rows,
        corner_of(0, (MID,), where, halos[:2]),
    )
    advance(planes, WIDE, v0, q0, s_wide, v1, q1)
    advance(planes, WIDE - 2, v1, q1, s_wide, v2, q2)
    advance(planes, WIDE - 4, v2, q2, s_wide, v3, q3)
    for i in range(planes):
        l = lap(v3, i + 2, OWN)
        now = s[i] * q3[i, OWN, :] + damping * l
        v_out[i] = v3[i + 2, OWN, :] + time_step * now
        q_out[i] = q3[i, OWN, :] + time_step * l
        moved = v[i] + v1[i + 6, OWN, :] + v2[i + 4, OWN, :] + v3[i + 2, OWN, :]
        u_out[i] = u[i] + time_step * moved
    pack_x((v_out, q_out), LATER, sends)


def last_steps(scale, u, v, q, s_wide, *rest):
    halos, (keep, send) = rest[:8], rest[8:10]
    v0, q0, v1, q1, v2, q2, rate, l7 = rest[10:]
    planes, _, _ = v.shape
    widen_moved((v0, q0), (v, q), halos)
    advance(planes, WIDE, v0, q0, s_wide, v1, q1)
    advance(planes, WIDE - 2, v1, q1, s_wide, v2, q2)
    count = planes + 4
    for i in range(count):
        edge = i < 2 or i >= count - 2
        rows = OWN if edge else ALL
        l = lap(v2, i + 2, rows)
        rate[i, rows, :] = s_wide[i + MID - 2, rows, :] * q2[i, rows, :] + damping * l
        if not edge:
            l7[i - 2] = l[OWN]
    for i in range(planes):
        l = lap(rate, i + 2, OWN)
        r = rate[i + 2, OWN, :]
        v7 = v2[i + 4, OWN, :]
        u8 = u[i] + time_step * (v[i] + v1[i + 6, OWN, :] + v7)
        v8 = v7 + time_step * r
        more = s_wide[i + MID, OWN, :] * l7[i] + damping * l
        keep[i] = u8 + scale[0] * r
        keep[planes + i] = v8 + scale[0] * more
        send[i] = u8 + scale[1] * r
        send[planes + i] = v8 + scale[1] * more


def join(h, keep, got, out_u, out_v):
    planes, rows, _ = out_u.shape
    half = rows // 2
    own = pl.ds(pl.multiple_of(h[0] * half, TILE), half)
    other = pl.ds(pl.multiple_of((1 - h[0]) * half, TILE), half)
    for k, out in enumerate((out_u, out_v)):
        part = pl.ds(k * planes, planes)
        out[:, own, :] = keep[part]
        out[:, other, :] = got[part]


def ring(count, step):
    return [(i, (i + step) % count) for i in range(count)]


def strips(gy, step):
    def place(t):
        j, h = divmod(t % (2 * gy), 2)
        return ((h + j) % 2) * gy + j

    return [(place(t), place(t + step)) for t in range(2 * gy)]


STARTS = ("a_up", "a_down", "b_up", "b_down", "y_up", "y_down", "c_up", "c_down")
STARTS_FIRST = ("a_up", "a_down", "y_up", "y_down", "s_up", "s_down")


def move(name, sent):
    step = 1 if name.endswith("up") else -1
    if name.startswith(("y", "c")):
        return lax.ppermute(sent, ("level", "gy"), strips(lax.axis_size("gy"), step))
    return lax.ppermute(sent, "gx", ring(lax.axis_size("gx"), step))


def exchange_first(sends):
    return [move(name, sent) for name, sent in zip(STARTS_FIRST, sends)]


def exchange(v, q, sends, extra):
    planes, _, depth = v.shape
    xla, xha, xlb, xhb = (move(name, sent) for name, sent in zip(STARTS, sends))
    count = 2 * planes
    if extra:
        count = corner_layout((MID,), count)[1]
    y = spec(count, TILE, depth)
    y_up, y_down = call(pack_rows, [y, y], (v, q, *extra))
    yl, yh = move("y_up", y_up), move("y_down", y_down)
    c = spec(corner_layout(LATER)[1], TILE, depth)
    c_up, c_down = call(pack_corners, [c, c], (xla, xha))
    return yl, yh, xla, xha, xlb, xhb, move("c_up", c_up), move("c_down", c_down)


def edge_specs(depth, widths):
    return [spec(len(part), TILE, depth) for part in x_layout(widths) for _ in range(2)]


def body(u, v, s):
    planes, rows, depth = u.shape
    half = rows // 2
    assert lax.axis_size("level") == 2 and planes >= WIDE and half == 2 * TILE
    level = lax.axis_index("level")
    h = ((level + lax.axis_index("gy")) % 2).astype(jnp.int32).reshape(1)
    mine = jnp.where(level == 0, 0.0, second).astype(jnp.float32)
    scale = jnp.stack([mine, second - mine])

    tall = half + 2 * TILE
    block = spec(planes, half, depth)
    wide, mid, thin, slim, bare = ((planes + 2 * w, tall, depth) for w in (WIDE, MID, 4, 2, 0))
    work = 100 * u.size
    sent = edge_specs(depth, LATER)

    x, y, xs = spec(4, half, depth), spec(planes * 3 // 2, TILE, depth), spec(MID, half, depth)
    outs = [block] * 3 + [x, x, y, y, xs, xs]
    u, v, s, *sends = pl.pallas_call(
        load_first,
        out_shape=outs,
        in_specs=[SMEM] + [pl.BlockSpec(memory_space=pltpu.HBM)] * 3,
        out_specs=[VMEM] * len(outs),
        scratch_shapes=[pltpu.SemaphoreType.DMA((3,))],
        compiler_params=pltpu.CompilerParams(vmem_limit_bytes=14 << 20),
    )(h, *(pltpu.with_memory_space_constraint(f, pltpu.HBM) for f in (u, v, s)))
    xl, xh, yl, yh, xsl, xsh = exchange_first(sends)
    args = (u, v, s, yl, yh, xl, xh)
    u, v, q, *sends = call(first_step, [block] * 3 + sent, args, (), (slim, slim), work)
    halos = exchange(v, q, sends, (xsl, xsh))
    u, v, q, s_wide, *sends = call(
        middle_steps,
        [block] * 3 + [spec(*mid)] + sent,
        (u, v, q, s, *halos, yl, yh, xsl, xsh),
        (),
        (wide, mid, mid, thin, thin, slim, slim, bare),
        work,
    )
    halos = exchange(v, q, sends, ())
    both = spec(2 * planes, half, depth)
    keep, send = call(
        last_steps,
        [both, both],
        (u, v, q, s_wide, *halos),
        (scale,),
        (wide, mid, mid, thin, thin, slim, slim, (planes, half, depth)),
        work,
    )
    got = lax.ppermute(send, "level", ring(2, 1))
    out_u, out_v = call(join, [spec(planes, rows, depth)] * 2, (keep, got), (h,))
    return out_u[None], out_v[None]


def solution(mesh):
    placed = (P("gx", "gy", None),) * 3
    return jax.shard_map(
        body,
        mesh=mesh,
        in_specs=placed,
        out_specs=(P("level", "gx", "gy", None), P("level", "gx", "gy", None)),
        check_vma=False,
    )
```

```python
import functools

import jax
import jax.numpy as jnp
from jax import lax
from jax.experimental import pallas as pl
from jax.experimental.pallas import tpu as pltpu
from jax.sharding import PartitionSpec as P


STEPS = 8

time_step = 0.12
damping = 0.05
second = 0.5 * STEPS * time_step * time_step

NEAR = 4.0 / 3.0
FAR = -1.0 / 12.0

TILE = 8
WIDE = 8
MID = 6
LAST = ((WIDE, 1), (MID, 1))
SECOND = LAST + ((MID, 3),)
EARLY = 20

VMEM = pl.BlockSpec(memory_space=pltpu.VMEM)
SMEM = pl.BlockSpec(memory_space=pltpu.SMEM)
OWN = slice(TILE, 3 * TILE)
ALL = slice(0, 4 * TILE)


def spec(*shape):
    return jax.ShapeDtypeStruct(shape, jnp.float32)


def call(kernel, outs, args, scalars=(), scratch=(), flops=0):
    moved = 4 * (sum(a.size for a in args) + sum(o.size for o in outs))
    return pl.pallas_call(
        kernel,
        out_shape=outs,
        in_specs=[SMEM] * len(scalars) + [VMEM] * len(args),
        out_specs=[VMEM] * len(outs),
        scratch_shapes=[pltpu.VMEM(shape, jnp.float32) for shape in scratch],
        compiler_params=pltpu.CompilerParams(vmem_limit_bytes=14 << 20),
        cost_estimate=pl.CostEstimate(flops=flops, bytes_accessed=moved, transcendentals=0),
    )(*scalars, *args)


def upper():
    return lax.broadcasted_iota(jnp.int32, (TILE, 1), 0) < TILE // 2


def lap(ref, i, rows):
    full = ref[i]
    count, depth = full.shape
    w = full[rows]
    near = ref[i - 1, rows, :] + ref[i + 1, rows, :]
    far = ref[i - 2, rows, :] + ref[i + 2, rows, :]
    near += pltpu.roll(w, 1, 1) + pltpu.roll(w, depth - 1, 1)
    far += pltpu.roll(w, 2, 1) + pltpu.roll(w, depth - 2, 1)
    near += pltpu.roll(full, 1, 0)[rows] + pltpu.roll(full, count - 1, 0)[rows]
    far += pltpu.roll(full, 2, 0)[rows] + pltpu.roll(full, count - 2, 0)[rows]
    return -7.5 * w + NEAR * near + FAR * far


def beyond(width, d):
    return max(0, width - 2 * ((d + 1) // 2))


def x_layout(fields):
    first, rest = {}, []
    for k, (width, nearest) in enumerate(fields):
        for d in range(nearest, width + 1):
            for part, least in (("A", 0), ("B", TILE // 2)):
                if beyond(width, d) > least:
                    first[k, d, part] = len(first)
                else:
                    rest.append((k, d, part))
    while len(first) < EARLY + (4 if len(fields) > 2 else 0):
        first[rest.pop(0)] = len(first)
    return first, {key: at for at, key in enumerate(rest)}


def corner_layout(fields):
    where, at = {}, 0
    for k, (width, _) in enumerate(fields):
        for d in range(1, width + 1):
            rows = beyond(width, d)
            if rows > TILE // 2:
                where[k, d], at = at, at + 2
            elif rows > TILE // 4 or (rows > 0 and d % 2):
                where[k, d], at = at, at + 1
            elif rows > 0:
                where[k, d] = where[k, d - 1]
    return where, at


def share(tiles, last):
    size = TILE // len(tiles)
    group = lax.broadcasted_iota(jnp.int32, (TILE, 1), 0) // size
    out = tiles[0]
    for n, tile in enumerate(tiles):
        if n and last:
            out = jnp.where(group == len(tiles) - 1 - n, pltpu.roll(tile, TILE - size * n, 0), out)
        elif n:
            out = jnp.where(group == n, pltpu.roll(tile, size * n, 0), out)
    return out


def unshare(tile, count, n, last):
    turn = TILE // count * n
    return pltpu.roll(tile, turn if last else TILE - turn, 0) if n else tile


def pack_edges(blocks, fields, sends):
    a_up, a_down, y_up, y_down, b_up, b_down = sends
    first, rest = x_layout(fields)
    for k, (f, (width, nearest)) in enumerate(zip(blocks, fields)):
        planes = f.shape[0]
        for d in range(nearest, width + 1):
            for plane, xa, xb in ((planes - d, a_up, b_up), (d - 1, a_down, b_down)):
                low, high = f[plane, 0:TILE, :], f[plane, TILE:, :]
                for part, tile in (
                    ("A", jnp.where(upper(), low, high)),
                    ("B", jnp.where(upper(), high, low)),
                ):
                    if (k, d, part) in first:
                        xa[first[k, d, part]] = tile
                    else:
                        xb[rest[k, d, part]] = tile
        if k < len(LAST):
            y_up[pl.ds(k * planes, planes)] = f[:, TILE:, :]
            y_down[pl.ds(k * planes, planes)] = f[:, 0:TILE, :]


def pack_corners(fields, xla, xha, *rest):
    earlier, (c_up, c_down) = rest[:-2], rest[-2:]
    first, _ = x_layout(fields)
    where, _ = corner_layout(fields)

    def tile(side, k, d):
        if (k, d, "A") in first:
            return (xla, xha)[side][first[k, d, "A"]]
        f, i = earlier[side], (earlier[0].shape[0] - d, 4 + d - 1)[side]
        return jnp.where(upper(), f[i, 0:TILE, :], f[i, TILE:, :])

    for (k, d), at in where.items():
        rows = beyond(fields[k][0], d)
        if rows > TILE // 2:
            for side, x in ((0, xla), (1, xha)):
                a, b = tile(side, k, d), x[first[k, d, "B"]]
                c_up[at + side] = jnp.where(upper(), b, a)
                c_down[at + side] = jnp.where(upper(), a, b)
        elif rows > TILE // 4 or d % 2:
            more = (d,) if rows > TILE // 4 else (d, d + 1)
            tiles = [tile(side, k, e) for side in (0, 1) for e in more]
            c_up[at] = share(tiles, True)
            c_down[at] = share(tiles, False)


def widen(out, width, centre, y_tile, x_tiles, corner):
    planes, _, depth = centre.shape
    for i in range(planes):
        out[width + i, 0:TILE, :] = y_tile(0, i)
        out[width + i, OWN, :] = centre[i]
        out[width + i, 3 * TILE :, :] = y_tile(1, i)
    for d in range(1, width + 1):
        for side, to in ((0, width - d), (1, width + planes - 1 + d)):
            low, high = x_tiles(side, d)
            out[to, TILE : 2 * TILE, :] = low
            out[to, 2 * TILE : 3 * TILE, :] = high
            if beyond(width, d) > 0:
                out[to, 0:TILE, :] = corner(side, 0, d)
                out[to, 3 * TILE :, :] = corner(side, 1, d)
            else:
                out[to, 0:TILE, :] = jnp.zeros((TILE, depth), jnp.float32)
                out[to, 3 * TILE :, :] = jnp.zeros((TILE, depth), jnp.float32)


def corner_of(k, fields, c):
    where, _ = corner_layout(fields)
    width = fields[k][0]

    def corner(side, y_side, d):
        tile, rows = where[k, d], beyond(width, d)
        if rows > TILE // 2:
            return c[y_side][tile + side]
        if rows > TILE // 4:
            return unshare(c[y_side][tile], 2, side, y_side == 0)
        return unshare(c[y_side][tile], 4, 2 * side + (d - 1) % 2, y_side == 0)

    return corner


def tiles_of(k, fields, xa, xb):
    first, rest = x_layout(fields)

    def tile(side, key):
        return xa[side][first[key]] if key in first else xb[side][rest[key]]

    def x_tiles(side, d):
        a, b = tile(side, (k, d, "A")), tile(side, (k, d, "B"))
        return jnp.where(upper(), a, b), jnp.where(upper(), b, a)

    return x_tiles


def widen_moved(outs, blocks, fields, halos):
    xa, y, xb, c = (halos[i : i + 2] for i in range(0, 8, 2))
    planes = blocks[0].shape[0]
    for k, (out, f) in enumerate(zip(outs, blocks)):
        widen(
            out,
            fields[k][0],
            f,
            lambda side, i: y[side][k * planes + i],
            tiles_of(k, fields, xa, xb),
            corner_of(k, fields, c),
        )


def load_first(h, u, v, s, u_own, v_own, s_own, *rest):
    x_up, x_down, y_up, y_down, sems = rest
    planes, half, _ = u_own.shape
    own = pl.ds(pl.multiple_of(h[0] * half, TILE), half)
    fields = (u_own, v_own, s_own)
    copies = [
        pltpu.make_async_copy(f.at[:, own, :], to, sems.at[k])
        for k, (f, to) in enumerate(zip((u, v, s), fields))
    ]
    for copy in copies:
        copy.start()
    for copy in copies:
        copy.wait()
    for k, f in enumerate(fields):
        x_up[pl.ds(2 * k, 2)] = f[planes - 2 :]
        x_down[pl.ds(2 * k, 2)] = f[0:2]
    pairs = planes // 2
    for i in range(pairs):
        shared = (u_own, i), (v_own, i), (u_own, i + pairs), (v_own, i + pairs)
        y_up[i] = share([f[plane, TILE:, :] for f, plane in shared], True)
        y_down[i] = share([f[plane, 0:TILE, :] for f, plane in shared], False)
    y_up[pairs:] = s_own[:, TILE:, :]
    y_down[pairs:] = s_own[:, 0:TILE, :]


def first_step(u, v, s, yl, yh, xl, xh, u_out, v_out, q_out, *rest):
    sends, (u0, v0) = rest[:6], rest[6:]
    planes, _, _ = u.shape
    pairs = planes // 2
    for k, (f, out) in enumerate(((u, u0), (v, v0))):
        out[pl.ds(2, planes), OWN, :] = f[...]
        out[0:2, OWN, :] = xl[pl.ds(2 * k, 2)]
        out[planes + 2 :, OWN, :] = xh[pl.ds(2 * k, 2)]
        for i in range(planes):
            n = k + 2 * (i // pairs)
            below = unshare(yl[i % pairs], 4, n, True)
            above = unshare(yh[i % pairs], 4, n, False)
            out[2 + i, 0:TILE, :] = below
            out[2 + i, 3 * TILE :, :] = above
    for i in range(planes):
        q, l = lap(u0, i + 2, OWN), lap(v0, i + 2, OWN)
        u_out[i] = u[i] + time_step * v[i]
        v_out[i] = v[i] + time_step * (s[i] * q + damping * l)
        q_out[i] = q + time_step * l
    pack_edges((v_out, q_out, s), SECOND, sends)


def advance(planes, width, v, q, s, v_out, q_out):
    count = planes + 2 * width - 4
    for i in range(count):
        edge = i < 2 or i >= count - 2
        rows = OWN if edge else ALL
        l = lap(v, i + 2, rows)
        now = s[i + MID + 2 - width, rows, :] * q[i, rows, :] + damping * l
        v_out[i, rows, :] = v[i + 2, rows, :] + time_step * now
        if not edge:
            q_out[i - 2] = q[i] + time_step * l


def middle_steps(u, v, q, s, *rest):
    halos, (ysl, ysh, xsl, xsh), rest = rest[:8], rest[8:12], rest[12:]
    (u_out, v_out, q_out, s_wide), sends = rest[:4], rest[4:10]
    v0, q0, v1, q1, v2, q2, v3, q3 = rest[10:]
    planes, _, _ = v.shape
    moved = tiles_of(2, SECOND, halos[0:2], halos[4:6])

    def s_rows(side, d):
        if d >= SECOND[2][1]:
            return moved(side, d)
        f, i = ((xsl, xsl.shape[0] - d), (xsh, 4 + d - 1))[side]
        return f[i, 0:TILE, :], f[i, TILE:, :]

    widen_moved((v0, q0), (v, q), SECOND, halos)
    widen(
        s_wide,
        MID,
        s,
        lambda side, i: (ysl, ysh)[side][planes // 2 + i],
        s_rows,
        corner_of(2, SECOND, halos[6:8]),
    )
    advance(planes, WIDE, v0, q0, s_wide, v1, q1)
    advance(planes, WIDE - 2, v1, q1, s_wide, v2, q2)
    advance(planes, WIDE - 4, v2, q2, s_wide, v3, q3)
    for i in range(planes):
        l = lap(v3, i + 2, OWN)
        now = s[i] * q3[i, OWN, :] + damping * l
        v_out[i] = v3[i + 2, OWN, :] + time_step * now
        q_out[i] = q3[i, OWN, :] + time_step * l
        moved = v[i] + v1[i + 6, OWN, :] + v2[i + 4, OWN, :] + v3[i + 2, OWN, :]
        u_out[i] = u[i] + time_step * moved
    pack_edges((v_out, q_out), LAST, sends)


def last_steps(scale, u, v, q, s_wide, *rest):
    halos, (keep, send) = rest[:8], rest[8:10]
    v0, q0, v1, q1, v2, q2, rate, l7 = rest[10:]
    planes, _, _ = v.shape
    widen_moved((v0, q0), (v, q), LAST, halos)
    advance(planes, WIDE, v0, q0, s_wide, v1, q1)
    advance(planes, WIDE - 2, v1, q1, s_wide, v2, q2)
    count = planes + 4
    for i in range(count):
        edge = i < 2 or i >= count - 2
        rows = OWN if edge else ALL
        l = lap(v2, i + 2, rows)
        rate[i, rows, :] = s_wide[i + MID - 2, rows, :] * q2[i, rows, :] + damping * l
        if not edge:
            l7[i - 2] = l[OWN]
    for i in range(planes):
        l = lap(rate, i + 2, OWN)
        r = rate[i + 2, OWN, :]
        v7 = v2[i + 4, OWN, :]
        u8 = u[i] + time_step * (v[i] + v1[i + 6, OWN, :] + v7)
        v8 = v7 + time_step * r
        more = s_wide[i + MID, OWN, :] * l7[i] + damping * l
        keep[i] = u8 + scale[0] * r
        keep[planes + i] = v8 + scale[0] * more
        send[i] = u8 + scale[1] * r
        send[planes + i] = v8 + scale[1] * more


def join(h, keep, got, out_u, out_v):
    planes, rows, _ = out_u.shape
    half = rows // 2
    own = pl.ds(pl.multiple_of(h[0] * half, TILE), half)
    other = pl.ds(pl.multiple_of((1 - h[0]) * half, TILE), half)
    for k, out in enumerate((out_u, out_v)):
        part = pl.ds(k * planes, planes)
        out[:, own, :] = keep[part]
        out[:, other, :] = got[part]


def ring(count, step):
    return [(i, (i + step) % count) for i in range(count)]


def strips(gy, step):
    def place(t):
        j, h = divmod(t % (2 * gy), 2)
        return ((h + j) % 2) * gy + j

    return [(place(t), place(t + step)) for t in range(2 * gy)]


STARTS = ("a_up", "a_down", "y_up", "y_down", "b_up", "b_down", "c_up", "c_down")


def move(name, sent):
    step = 1 if name.endswith("up") else -1
    if name.startswith(("y", "c")):
        return lax.ppermute(sent, ("level", "gy"), strips(lax.axis_size("gy"), step))
    return lax.ppermute(sent, "gx", ring(lax.axis_size("gx"), step))


def exchange(fields, sends, earlier):
    got = [move(name, sent) for name, sent in zip(STARTS, sends)]
    if fields:
        c = spec(corner_layout(fields)[1], TILE, sends[0].shape[-1])
        kernel = functools.partial(pack_corners, fields)
        corners = call(kernel, [c, c], (got[0], got[1], *earlier))
        got += [move(name, sent) for name, sent in zip(STARTS[6:], corners)]
    return got


def edge_specs(planes, depth, fields):
    first, rest = x_layout(fields)
    return [spec(n, TILE, depth) for n in (len(first), 2 * planes, len(rest)) for _ in range(2)]


def body(u, v, s):
    planes, rows, depth = u.shape
    half = rows // 2
    assert lax.axis_size("level") == 2 and planes >= WIDE and half == 2 * TILE
    level = lax.axis_index("level")
    h = ((level + lax.axis_index("gy")) % 2).astype(jnp.int32).reshape(1)
    mine = jnp.where(level == 0, 0.0, second).astype(jnp.float32)
    scale = jnp.stack([mine, second - mine])

    tall = half + 2 * TILE
    block = spec(planes, half, depth)
    wide, mid, thin, slim, bare = ((planes + 2 * w, tall, depth) for w in (WIDE, MID, 4, 2, 0))
    work = 100 * u.size

    x, y = spec(6, half, depth), spec(planes * 3 // 2, TILE, depth)
    outs = [block] * 3 + [x, x, y, y]
    u, v, s, *sends = pl.pallas_call(
        load_first,
        out_shape=outs,
        in_specs=[SMEM] + [pl.BlockSpec(memory_space=pltpu.HBM)] * 3,
        out_specs=[VMEM] * len(outs),
        scratch_shapes=[pltpu.SemaphoreType.DMA((3,))],
        compiler_params=pltpu.CompilerParams(vmem_limit_bytes=14 << 20),
    )(h, *(pltpu.with_memory_space_constraint(f, pltpu.HBM) for f in (u, v, s)))
    xl, xh, yl, yh = exchange((), sends, ())
    sent = edge_specs(planes, depth, SECOND)
    args = (u, v, s, yl, yh, xl, xh)
    u, v, q, *sends = call(first_step, [block] * 3 + sent, args, (), (slim, slim), work)
    halos = exchange(SECOND, sends, (xl, xh))
    sent = edge_specs(planes, depth, LAST)
    u, v, q, s_wide, *sends = call(
        middle_steps,
        [block] * 3 + [spec(*mid)] + sent,
        (u, v, q, s, *halos, yl, yh, xl, xh),
        (),
        (wide, mid, mid, thin, thin, slim, slim, bare),
        work,
    )
    halos = exchange(LAST, sends, ())
    both = spec(2 * planes, half, depth)
    keep, send = call(
        last_steps,
        [both, both],
        (u, v, q, s_wide, *halos),
        (scale,),
        (wide, mid, mid, thin, thin, slim, slim, (planes, half, depth)),
        work,
    )
    got = lax.ppermute(send, "level", ring(2, 1))
    out_u, out_v = call(join, [spec(planes, rows, depth)] * 2, (keep, got), (h,))
    return out_u[None], out_v[None]


def solution(mesh):
    placed = (P("gx", "gy", None),) * 3
    return jax.shard_map(
        body,
        mesh=mesh,
        in_specs=placed,
        out_specs=(P("level", "gx", "gy", None), P("level", "gx", "gy", None)),
        check_vma=False,
    )
```
